32 devices in a mesh: fsdp: 4 (over y, x), ctx: 4 (over z), tensor: 2 (over core).
Axes of the slice: x: 2, y: 2, z: 4, core: 2. Of those that a mesh axis runs over, the one named last changes fastest.
Arguments:
- layer_input: bfloat16 [8, 1024, 768], P(('fsdp', 'tensor'), 'ctx'), may hold values from -6 to 6
- cotangent: bfloat16 [8, 1024, 768], P(('fsdp', 'tensor'), 'ctx'), may hold values from -6 to 6
- segment_ids: int32 [8, 1024], P(('fsdp', 'tensor'), 'ctx'), may hold values from 0 to 5, as said below
- positions: int32 [8, 1024], P(('fsdp', 'tensor'), 'ctx'), may hold values from 0 to 1023, as said below
- query_key_value_weight: bfloat16 [768, 2304], P('fsdp'), may hold values from -0.21875 to 0.21875
- projection_matrix: bfloat16 [768, 768], P('fsdp'), may hold values from -0.875 to 0.875
- up_matrix: bfloat16 [768, 3072], P('fsdp', 'tensor'), may hold values from -0.21875 to 0.21875
- down_matrix: bfloat16 [3072, 768], P('tensor', 'fsdp'), may hold values from -0.109375 to 0.109375
- attn_gain: bfloat16 [768], P('fsdp'), may hold values from 0.5 to 1.5
- attn_shift: bfloat16 [768], P('fsdp'), may hold values from -3 to 3
- ffn_gain: bfloat16 [768], P('fsdp'), may hold values from 0.5 to 1.5
- ffn_shift: bfloat16 [768], P('fsdp'), may hold values from -3 to 3
- out_bias: bfloat16 [768], P('fsdp'), may hold values from -3 to 3
- up_projection_bias: bfloat16 [3072], P('fsdp'), may hold values from -3 to 3
Outputs:
- layer_output: bfloat16 [8, 1024, 768], P(('fsdp', 'tensor'), 'ctx')
- input_grad: float32 [8, 1024, 768], P(('fsdp', 'tensor'), 'ctx')
- qkv_grad: float32 [768, 2304], P('fsdp')
- proj_grad: float32 [768, 768], P('fsdp')
- up_grad: float32 [768, 3072], P('fsdp', 'tensor')
- down_grad: float32 [3072, 768], P('tensor', 'fsdp')
- attn_gain_grad: float32 [768], P('fsdp')
- attn_shift_grad: float32 [768], P('fsdp')
- ffn_gain_grad: float32 [768], P('fsdp')
- ffn_shift_grad: float32 [768], P('fsdp')
- out_bias_grad: float32 [768], P('fsdp')
- up_bias_grad: float32 [3072], P('fsdp')
The draws below stay inside these ranges and needn't reach their ends.
Inputs may be any that keep to these rules, and one draw needn't show every extreme that they name: `segment_ids`: along each sequence the ids start at 0 and rise by one at each document's first token; every document has 200 to 1024 tokens, except the last one of a sequence, which the sequence's end may cut. `positions`: each document's tokens count 0, 1, 2, ... from its first token, which starts with the segment_ids' change.
All inputs are finite; a program needn't handle non-finite values.
Results may differ from the reference program's by a relative error of at most 0.018.
Values may be sent and summed in bfloat16 or wider, within the bound.
No kernel may reach another device: no remote copies, remote signals or barrier semaphores. Data moves between devices by JAX's collectives and lax.ppermute only.
A program may use at most 192 MiB of HBM per device.

```python
import math
import jax
import jax.numpy as jnp
from jax import lax

D = 768
HEADS = 12
HEAD = 64
ROT = 16
FF = 3072
LEN = 1024
DOC_MIN = 200
DOC_MAX = 1024
SEQS = 8


def documents(key):
    most_docs = LEN // DOC_MIN + 1
    lengths = jax.random.randint(jax.random.fold_in(key, 7), (SEQS, most_docs), DOC_MIN, DOC_MAX + 1)
    lengths = lengths.at[0, 0].set(DOC_MAX)
    lengths = lengths.at[1, :].set(DOC_MIN)
    doc_ends = jnp.cumsum(lengths, axis=1)
    doc_starts = doc_ends - lengths
    token_index = jnp.arange(LEN)
    segment = jnp.sum((token_index[None, :, None] >= doc_ends[:, None, :]).astype(jnp.int32), axis=2)
    onehot = (segment[:, :, None] == jnp.arange(most_docs)[None, None, :]).astype(jnp.int32)
    doc_first = jnp.sum(onehot * doc_starts[:, None, :], axis=2)
    return (segment.astype(jnp.int32), (token_index[None, :] - doc_first).astype(jnp.int32))


def draw_segment_ids(key, part):
    return documents(key)[0]


def draw_positions(key, part):
    return documents(key)[1]


def shard_levels(rng, dims, pieces, low, high):
    level, own = 1.0, jax.random.fold_in(rng, 6)
    for axis_at, shards_of in pieces:
        steps = jnp.exp(jax.random.uniform(jax.random.fold_in(own, axis_at), (shards_of,), jnp.float32, low / len(pieces), high / len(pieces)))
        level = level * jnp.repeat(steps, dims[axis_at] // shards_of).reshape([-1 if axis == axis_at else 1 for axis in range(len(dims))])
    return level


def gaussian(own_key, extent, scale, limit, shards=(), held_as=jnp.bfloat16):
    values = jax.random.normal(own_key, extent, jnp.float32) * scale
    if len(shards) > 0:
        values = shard_levels(own_key, extent, shards, -0.22, 0.18) * values
    return jnp.clip(values, min=-limit, max=limit).astype(held_as)


def setup_inputs(seed: int = 0) -> dict:
    key_of = jax.random.split(jax.random.key(seed), 15)
    layer_input = gaussian(key_of[0], (SEQS, LEN, D), 1.0, 6.0, ((0, 8), (1, 4)))
    cotangent = gaussian(key_of[1], (SEQS, LEN, D), 1.0, 6.0, ((0, 8), (1, 4)))
    segment_ids = draw_segment_ids(jax.random.fold_in(key_of[14], 71), 0)
    positions = draw_positions(jax.random.fold_in(key_of[14], 71), 0)
    query_key_value_weight = gaussian(key_of[4], (D, 3 * D), D ** -0.5, 0.21875, ((0, 4),))
    projection_matrix = gaussian(key_of[5], (D, D), (D // 16) ** -0.5, 0.875, ((0, 4),))
    up_matrix = gaussian(key_of[6], (D, FF), D ** -0.5, 0.21875, ((0, 4), (1, 2)))
    down_matrix = gaussian(key_of[7], (FF, D), FF ** -0.5, 0.109375, ((0, 2), (1, 4)))
    attn_gain = jnp.clip(1.0 + 0.1 * jax.random.normal(key_of[8], (D,), jnp.float32), 0.5, 1.5).astype(jnp.bfloat16)
    attn_shift = gaussian(key_of[9], (D,), 0.5, 3.0, ((0, 4),))
    ffn_gain = jnp.clip(1.0 + 0.1 * jax.random.normal(key_of[10], (D,), jnp.float32), 0.5, 1.5).astype(jnp.bfloat16)
    ffn_shift = gaussian(key_of[11], (D,), 0.5, 3.0, ((0, 4),))
    out_bias = gaussian(key_of[12], (D,), 0.5, 3.0, ((0, 4),))
    up_projection_bias = gaussian(key_of[13], (FF,), 0.5, 3.0, ((0, 4),))
    return dict(layer_input=layer_input, cotangent=cotangent, segment_ids=segment_ids, positions=positions, query_key_value_weight=query_key_value_weight, projection_matrix=projection_matrix, up_matrix=up_matrix, down_matrix=down_matrix, attn_gain=attn_gain, attn_shift=attn_shift, ffn_gain=ffn_gain, ffn_shift=ffn_shift, out_bias=out_bias, up_projection_bias=up_projection_bias)


@jax.custom_vjp
def low(v):
    return lax.optimization_barrier(v.astype(jnp.bfloat16)).astype(jnp.float32)

@jax.custom_vjp
def lower_backward(v):
    return v

def low_keep(v):
    return (low(v), None)

def low_pass(kept, grad):
    return (grad,)

def back_keep(v):
    return (v, None)

def back_low(kept, grad):
    return (low(grad),)
low.defvjp(low_keep, low_pass)
lower_backward.defvjp(back_keep, back_low)
epsilon = 1e-05
masked_score = -1e+30

def norm_layer(values, gain_vec, shift_vec):
    center = lax.optimization_barrier(jnp.mean(values, axis=-1, keepdims=True))
    shifted = values - center
    spread = lax.optimization_barrier(jnp.mean(shifted * shifted, axis=-1, keepdims=True))
    return shifted * lax.rsqrt(spread + epsilon) * gain_vec + shift_vec

def rotary_tables(positions):
    half_rot = ROT // 2
    frequency = 10000.0 ** (-(2.0 * jnp.arange(half_rot, dtype=jnp.float32)) / ROT)
    angles = positions.astype(jnp.float32)[..., None] * frequency
    return (jnp.cos(angles), jnp.sin(angles))

def rotate(fields, cosine, sine_tab):
    half_rot = ROT // 2
    first_half = fields[..., :half_rot]
    second = fields[..., half_rot:ROT]
    return jnp.concatenate([first_half * cosine - second * sine_tab, second * cosine + first_half * sine_tab, fields[..., ROT:]], axis=-1)

def attend(queries, key_heads, values, segment):
    scores = jnp.einsum('qhe,khe->hqk', queries, key_heads, precision=lax.Precision.HIGHEST) / math.sqrt(HEAD)
    scores = lower_backward(scores)
    row_ids = jnp.arange(LEN)
    allowed = (segment[:, None] == segment[None, :]) & (row_ids[None, :] <= row_ids[:, None])
    attn_probs = low(jax.nn.softmax(jnp.where(allowed[None], scores, masked_score), axis=-1))
    return jnp.einsum('hqk,khe->qhe', attn_probs, values, precision=lax.Precision.HIGHEST)

def attend_members(members):
    return attend(members[0], members[1], members[2], members[3])

def layer(inputs, query_key_value_weight, projection_matrix, up_matrix, down_matrix, attn_gain, attn_shift, ffn_gain, ffn_shift, out_bias, up_projection_bias, cosine, sine_tab, segment):
    group_size = inputs.shape[0]
    first_hidden = low(norm_layer(inputs, attn_gain, attn_shift))
    second_hidden = low(norm_layer(inputs, ffn_gain, ffn_shift))
    projected_output = lower_backward(jnp.einsum('mwe,eo->mwo', first_hidden, query_key_value_weight, precision=lax.Precision.HIGHEST))
    projected_output = projected_output.reshape(group_size, LEN, 3, HEADS, HEAD)
    queries = lower_backward(low(rotate(projected_output[:, :, 0], cosine, sine_tab)))
    key_heads = lower_backward(low(rotate(projected_output[:, :, 1], cosine, sine_tab)))
    values = lower_backward(low(projected_output[:, :, 2]))
    context_rows = lax.map(jax.checkpoint(attend_members), (queries, key_heads, values, segment))
    context_rows = lower_backward(low(context_rows)).reshape(group_size, LEN, D)
    attention_branch = jnp.einsum('onq,qb->onb', context_rows, projection_matrix, precision=lax.Precision.HIGHEST)
    preactivation = lower_backward(jnp.einsum('xyp,pe->xye', second_hidden, up_matrix, precision=lax.Precision.HIGHEST) + up_projection_bias)
    activated_hidden = low(jax.nn.gelu(preactivation, approximate=False))
    feedforward_output = jnp.einsum('kpq,qg->kpg', activated_hidden, down_matrix, precision=lax.Precision.HIGHEST)
    return inputs + attention_branch + feedforward_output + out_bias

def reference(layer_input, cotangent, segment_ids, positions, query_key_value_weight, projection_matrix, up_matrix, down_matrix, attn_gain, attn_shift, ffn_gain, ffn_shift, out_bias, up_projection_bias):
    weights = tuple((member.astype(jnp.float32) for member in (query_key_value_weight, projection_matrix, up_matrix, down_matrix, attn_gain, attn_shift, ffn_gain, ffn_shift, out_bias, up_projection_bias)))
    seq_total = layer_input.shape[0]
    group_size = math.gcd(seq_total, max(1, 4096 // LEN))
    step_count = seq_total // group_size

    def by_groups(array):
        return array.reshape((step_count, group_size) + array.shape[1:])
    cosine, sine_tab = rotary_tables(positions)
    scanned = (by_groups(layer_input.astype(jnp.float32)), by_groups(cotangent.astype(jnp.float32)), by_groups(segment_ids), by_groups(cosine[:, :, None]), by_groups(sine_tab[:, :, None]))

    def scan_step(running, members):
        inputs, grad_out, segment, cos_group, sin_group = members

        def forward(values, *params):
            return layer(values, *params, cos_group, sin_group, segment)
        output, pullback = jax.vjp(forward, inputs, *weights)
        gradients = pullback(grad_out)
        running = tuple((total_now + grad_now for total_now, grad_now in zip(running, gradients[1:])))
        return (running, (output, gradients[0]))
    zero_grads = tuple((jnp.zeros(member.shape, jnp.float32) for member in weights))
    totals, (outputs, grad_inputs) = lax.scan(scan_step, zero_grads, scanned)
    return (outputs.reshape(layer_input.shape).astype(jnp.bfloat16), grad_inputs.reshape(layer_input.shape), totals[0], totals[1], totals[2], totals[3], totals[4], totals[5], totals[6], totals[7], totals[8], totals[9])
```

```python
import math

import jax
import jax.numpy as jnp
from jax import lax
from jax.experimental import pallas as pl
from jax.experimental.pallas import tpu as pltpu
from jax.sharding import PartitionSpec as P

HEADS = 12
HEAD = 64
ROT = 16
FF = 3072

epsilon = 1e-05
masked_score = -1e30
bf16 = jnp.bfloat16
f32 = jnp.float32


def normalize(values):
    center = jnp.mean(values, axis=-1, keepdims=True)
    shifted = values - center
    spread = jnp.mean(shifted * shifted, axis=-1, keepdims=True)
    inverse = lax.rsqrt(spread + epsilon)
    return (shifted * inverse, inverse)


def mm(a, b, ca, cb):
    return lax.dot_general(a, b, (((ca,), (cb,)), ((), ())), preferred_element_type=f32)


def ring(size, step):
    return [(i, (i + step) % size) for i in range(size)]


def gather_pieces(piece, axis):
    size = lax.axis_size(axis)
    return [piece] + [lax.ppermute(piece, axis, ring(size, k)) for k in range(1, size)]


def in_order(pieces, axis):
    size = lax.axis_size(axis)
    own = lax.axis_index(axis)
    rows = pieces[0].shape[0]
    whole = jnp.zeros((size * rows,) + pieces[0].shape[1:], pieces[0].dtype)
    for k, piece in enumerate(pieces):
        place = lax.rem(own - k + size, size)
        whole = lax.dynamic_update_slice_in_dim(whole, piece, place * rows, 0)
    return whole


def scatter_total(parts, axis):
    size = lax.axis_size(axis)
    own = lax.axis_index(axis)
    rows = parts.shape[0] // size
    total = lax.dynamic_slice_in_dim(parts, own * rows, rows, 0).astype(f32)
    for k in range(1, size):
        place = lax.rem(own + k, size)
        block = lax.dynamic_slice_in_dim(parts, place * rows, rows, 0)
        total = total + lax.ppermute(block, axis, ring(size, k)).astype(f32)
    return total


def attention_kernel(qkv_ref, grad_ref, cos_ref, sin_ref, row_ref, col_ref, ctx_ref, out_ref):
    half = ROT // 2
    length = qkv_ref.shape[-1]
    block = min(256, length)
    cosine = cos_ref[...]
    sine = sin_ref[...]

    def rotated(fields, sign):
        first = fields[:half]
        second = fields[half:ROT]
        return jnp.concatenate(
            [
                first * cosine - sign * (second * sine),
                second * cosine + sign * (first * sine),
                fields[ROT:],
            ],
            axis=0,
        )

    scale = 1.0 / math.sqrt(HEAD)
    query = (rotated(qkv_ref[0, 0], 1.0).astype(bf16).astype(f32) * scale).astype(bf16)
    keys = rotated(qkv_ref[1, 0], 1.0).astype(bf16)
    values = qkv_ref[2, 0].astype(bf16)
    grads = grad_ref[0]
    grad_query = []
    grad_key = [None] * (length // block)
    grad_value = [None] * (length // block)
    for index in range(length // block):
        low = index * block
        high = low + block
        query_block = query[:, low:high]
        grad_block = grads[:, low:high]
        scores = mm(keys[:, :high], query_block, 0, 0)
        same_doc = col_ref[:high] == row_ref[:, low:high]
        key_ids = lax.broadcasted_iota(jnp.int32, (high, block), 0)
        query_ids = low + lax.broadcasted_iota(jnp.int32, (high, block), 1)
        allowed = same_doc & (key_ids <= query_ids)
        scores = jnp.where(allowed, scores, masked_score)
        peak = jnp.max(scores, axis=0, keepdims=True)
        terms = jnp.exp(scores - peak)
        probs = terms * (1.0 / jnp.sum(terms, axis=0, keepdims=True))
        probs_bf = probs.astype(bf16)
        ctx_ref[0, :, low:high] = mm(values[:, :high], probs_bf, 1, 0).astype(bf16)
        grad_probs = mm(values[:, :high], grad_block, 0, 0)
        delta = jnp.sum(probs * grad_probs, axis=0, keepdims=True)
        grad_scores = (probs * (grad_probs - delta)).astype(bf16)
        grad_query.append(mm(keys[:, :high], grad_scores, 1, 0) * scale)
        dk = mm(query_block, grad_scores, 1, 1)
        dv = mm(grad_block, probs_bf, 1, 1)
        for j in range(index + 1):
            part = slice(j * block, (j + 1) * block)
            grad_key[j] = dk[:, part] if grad_key[j] is None else grad_key[j] + dk[:, part]
            grad_value[j] = dv[:, part] if grad_value[j] is None else grad_value[j] + dv[:, part]
    out_ref[0, 0] = rotated(jnp.concatenate(grad_query, axis=1), -1.0).astype(bf16)
    out_ref[1, 0] = rotated(jnp.concatenate(grad_key, axis=1), -1.0).astype(bf16)
    out_ref[2, 0] = jnp.concatenate(grad_value, axis=1).astype(bf16)


def attend(qkv, grads, cosine, sine, segment):
    _, heads, head, length = qkv.shape
    whole = lambda shape: pl.BlockSpec(shape, lambda h: (0,) * len(shape))
    return pl.pallas_call(
        attention_kernel,
        grid=(heads,),
        in_specs=[
            pl.BlockSpec((3, 1, head, length), lambda h: (0, h, 0, 0)),
            pl.BlockSpec((1, head, length), lambda h: (h, 0, 0)),
            whole(cosine.shape),
            whole(sine.shape),
            whole((1, length)),
            whole((length, 1)),
        ],
        out_specs=[
            pl.BlockSpec((1, head, length), lambda h: (h, 0, 0)),
            pl.BlockSpec((3, 1, head, length), lambda h: (0, h, 0, 0)),
        ],
        out_shape=[
            jax.ShapeDtypeStruct((heads, head, length), bf16),
            jax.ShapeDtypeStruct((3, heads, head, length), bf16),
        ],
        name="attend",
    )(qkv, grads, cosine, sine, segment[None, :], segment[:, None])


def shards(
    layer_input,
    cotangent,
    segment_ids,
    positions,
    query_key_value_weight,
    projection_matrix,
    up_matrix,
    down_matrix,
    attn_gain,
    attn_shift,
    ffn_gain,
    ffn_shift,
    out_bias,
    up_projection_bias,
):
    fsdp_size = lax.axis_size("fsdp")
    ctx_size = lax.axis_size("ctx")
    tensor_size = lax.axis_size("tensor")
    ctx_own = lax.axis_index("ctx")
    tensor_own = lax.axis_index("tensor")
    _, piece_len, width = layer_input.shape
    seq_len = piece_len * ctx_size
    rows = query_key_value_weight.shape[0]
    head_count = HEADS // ctx_size
    head_width = head_count * HEAD
    half_tensor = FF // tensor_size
    units = half_tensor // ctx_size
    other_tensor = [(i, (i + 1) % tensor_size) for i in range(tensor_size)]

    qkv_own = lax.dynamic_slice_in_dim(
        query_key_value_weight.reshape(rows, 3, width), ctx_own * head_width, head_width, 2
    ).reshape(rows, 3 * head_width)
    up_own = lax.dynamic_slice_in_dim(up_matrix, ctx_own * units, units, 1)
    down_own = lax.dynamic_slice_in_dim(down_matrix, ctx_own * units, units, 0).T
    packed = jnp.concatenate([qkv_own, projection_matrix, up_own, down_own], axis=1)
    small = jnp.concatenate(
        [attn_gain, attn_shift, ffn_gain, ffn_shift, out_bias, up_projection_bias]
    )
    small_rows = 16
    small = jnp.pad(small, (0, small_rows * packed.shape[1] - small.shape[0]))
    packed = jnp.concatenate([packed, small.reshape(small_rows, -1)], axis=0)
    gathered = lax.all_gather(packed, "fsdp", axis=0, tiled=False)
    matrix = gathered[:, :rows].reshape(width, -1)
    edge = 3 * head_width
    qkv_w = matrix[:, :edge]
    proj_all = matrix[:, edge : edge + width]
    ffn_half = matrix[:, edge + width :]
    ffn_other = lax.ppermute(ffn_half, "tensor", other_tensor)
    up_w = jnp.concatenate([ffn_half[:, :units], ffn_other[:, :units]], axis=1)
    down_w = jnp.concatenate([ffn_half[:, units:], ffn_other[:, units:]], axis=1)
    proj_w = lax.dynamic_slice_in_dim(proj_all, ctx_own * head_width, head_width, 0)
    vectors = gathered[:, rows, :].astype(f32)
    take = lambda k: vectors[:, k * rows : (k + 1) * rows].reshape(width)
    gain_one, shift_one, gain_two, shift_two, bias_all = [take(k) for k in range(5)]
    up_bias = vectors[:, 5 * rows : 5 * rows + FF // fsdp_size].reshape(FF)
    unit_start = lambda t: t * half_tensor + ctx_own * units
    other_own = tensor_size - 1 - tensor_own
    bias_w = jnp.concatenate(
        [
            lax.dynamic_slice_in_dim(up_bias, unit_start(tensor_own), units, 0),
            lax.dynamic_slice_in_dim(up_bias, unit_start(other_own), units, 0),
        ]
    )

    position = positions.reshape(piece_len)
    meta = jnp.concatenate(
        [segment_ids.reshape(piece_len), position // 32, position % 32]
    ).astype(bf16)
    meta = jnp.pad(meta.reshape(1, -1), ((0, 15), (0, width - 3 * piece_len)))
    piece = layer_input.reshape(piece_len, width)
    pieces = gather_pieces(jnp.concatenate([piece, meta], axis=0), "ctx")
    cot_piece = cotangent.reshape(piece_len, width)
    barred = lax.optimization_barrier((cot_piece, *pieces))
    cot_piece, pieces = barred[0], barred[1:]
    grad_bf = in_order(gather_pieces(cot_piece, "ctx"), "ctx")
    tokens = in_order([item[:piece_len] for item in pieces], "ctx")
    labels = in_order([item[piece_len : piece_len + 1] for item in pieces], "ctx").astype(f32)
    segment = labels[:, :piece_len].reshape(seq_len)
    place = (labels[:, piece_len : 2 * piece_len] * 32 + labels[:, 2 * piece_len : 3 * piece_len]).reshape(seq_len)
    half_rot = ROT // 2
    frequency = 10000.0 ** (-(2.0 * jnp.arange(half_rot, dtype=f32)) / ROT)
    angles = frequency[:, None] * place[None, :]
    cosine = jnp.cos(angles)
    sine = jnp.sin(angles)

    normed, _ = normalize(tokens.astype(f32))
    first_hidden = (normed * gain_one + shift_one).astype(bf16)
    second_hidden = (normed * gain_two + shift_two).astype(bf16)

    pre = mm(second_hidden, up_w, 1, 0) + bias_w
    cdf = 0.5 * (1.0 + lax.erf(pre * (1.0 / math.sqrt(2.0))))
    act = (pre * cdf).astype(bf16)
    slope = (cdf + pre * (jnp.exp(-0.5 * pre * pre) * (1.0 / math.sqrt(2.0 * math.pi)))).astype(bf16)
    feed = mm(act, down_w, 1, 1)
    grad_pre = (mm(grad_bf, down_w, 1, 0) * slope.astype(f32)).astype(bf16)
    grad_two = mm(grad_pre, up_w, 1, 1)
    up_part = mm(second_hidden, grad_pre, 0, 0)
    down_part = mm(grad_bf, act, 0, 0)
    ffn_keep = jnp.concatenate([up_part[:, :units], down_part[:, :units]], axis=1)
    ffn_send = jnp.concatenate([up_part[:, units:], down_part[:, units:]], axis=1).astype(bf16)
    ffn_grad = (ffn_keep + lax.ppermute(ffn_send, "tensor", other_tensor).astype(f32)).astype(bf16)
    ffn_rows = lax.psum_scatter(ffn_grad, "fsdp", scatter_dimension=0, tiled=True)
    ffn_all = lax.all_gather(ffn_rows, "ctx", axis=0, tiled=False).astype(f32)
    up_grad = ffn_all[:, :, :units].transpose(1, 0, 2).reshape(rows, half_tensor)
    down_grad = ffn_all[:, :, units:].transpose(0, 2, 1).reshape(half_tensor, rows)

    qkv = mm(qkv_w, first_hidden, 0, 1).reshape(3, head_count, HEAD, seq_len)
    grad_context = mm(proj_w, grad_bf, 1, 1).astype(bf16).reshape(head_count, HEAD, seq_len)
    context, grad_projected = attend(qkv, grad_context, cosine, sine, segment)
    context = context.reshape(head_width, seq_len)
    grad_projected = grad_projected.reshape(3 * head_width, seq_len)
    out_part = (feed + mm(context, proj_w, 0, 0)).astype(bf16)
    out_sum = scatter_total(out_part, "ctx")
    output = piece.astype(f32) + out_sum + bias_all
    layer_output = output.astype(bf16)[None]

    grad_one = mm(grad_projected, qkv_w, 0, 1)
    mixed = (grad_one * gain_one + grad_two * gain_two).astype(bf16)
    scaled = scatter_total(mixed, "ctx")
    own_normed, own_inverse = normalize(piece.astype(f32))
    first_mean = jnp.mean(scaled, axis=-1, keepdims=True)
    second_mean = jnp.mean(scaled * own_normed, axis=-1, keepdims=True)
    cot_float = cot_piece.astype(f32)
    input_grad = cot_float + own_inverse * (scaled - first_mean - own_normed * second_mean)

    qkv_part = mm(first_hidden, grad_projected, 0, 1)
    proj_part = mm(grad_bf, context, 0, 1)
    bias_sum = jnp.sum(grad_pre.astype(f32), axis=0)
    bias_part = jnp.zeros((FF,), f32)
    bias_part = lax.dynamic_update_slice_in_dim(bias_part, bias_sum[:units], unit_start(tensor_own), 0)
    bias_part = lax.dynamic_update_slice_in_dim(bias_part, bias_sum[units:], unit_start(other_own), 0)
    small_part = jnp.stack(
        [
            jnp.sum(grad_one * normed, axis=0),
            jnp.sum(grad_one, axis=0),
            jnp.sum(grad_two * normed, axis=0),
            jnp.sum(grad_two, axis=0),
            jnp.sum(cot_float, axis=0),
        ],
        axis=1,
    )
    attn_part = jnp.concatenate(
        [qkv_part, proj_part, small_part, bias_part.reshape(width, FF // width)], axis=1
    )
    sub = rows // tensor_size
    attn_part = attn_part.reshape(fsdp_size, tensor_size, sub, -1)
    attn_keep = lax.dynamic_index_in_dim(attn_part, tensor_own, 1, keepdims=False)
    attn_send = lax.dynamic_index_in_dim(attn_part, other_own, 1, keepdims=False).astype(bf16)
    attn_grad = (attn_keep + lax.ppermute(attn_send, "tensor", other_tensor).astype(f32)).astype(bf16)
    attn_rows = lax.psum_scatter(attn_grad, "fsdp", scatter_dimension=0, tiled=False)
    attn_all = lax.all_gather(attn_rows, ("ctx", "tensor"), axis=0, tiled=False)
    attn_all = attn_all.reshape(ctx_size, rows, -1)
    qkv_grad = attn_all[:, :, :edge].astype(f32).reshape(ctx_size, rows, 3, head_width)
    qkv_grad = qkv_grad.transpose(1, 2, 0, 3).reshape(rows, 3 * width)
    proj_cols = attn_all[:, :, edge : edge + head_width].transpose(0, 2, 1).reshape(width, rows)
    proj_grad = lax.all_to_all(proj_cols.reshape(fsdp_size, rows, rows), "fsdp", 0, 0, tiled=True)
    proj_grad = proj_grad.transpose(1, 0, 2).reshape(rows, width).astype(f32)
    tail = jnp.sum(attn_all[:, :, edge + head_width :].astype(f32), axis=0)
    bias_grad = tail[:, 5:].reshape(FF // fsdp_size)
    return (
        layer_output,
        input_grad[None],
        qkv_grad,
        proj_grad,
        up_grad,
        down_grad,
        tail[:, 0],
        tail[:, 1],
        tail[:, 2],
        tail[:, 3],
        tail[:, 4],
        bias_grad,
    )


def solution(mesh):
    tokens = P(("fsdp", "tensor"), "ctx", None)
    labels = P(("fsdp", "tensor"), "ctx")
    weights = (P("fsdp", None), P("fsdp", None), P("fsdp", "tensor"), P("tensor", "fsdp"))
    vectors = (P("fsdp"),) * 6
    return jax.shard_map(
        shards,
        mesh=mesh,
        in_specs=(tokens, tokens, labels, labels) + weights + vectors,
        out_specs=(tokens, tokens) + weights + vectors,
        check_vma=False,
    )
```

```python
import math

import jax
import jax.numpy as jnp
from jax import lax
from jax.experimental import pallas as pl
from jax.experimental.pallas import tpu as pltpu
from jax.sharding import PartitionSpec as P

HEADS = 12
HEAD = 64
ROT = 16
FF = 3072

epsilon = 1e-05
masked_score = -1e30
bf16 = jnp.bfloat16
f32 = jnp.float32


def normalize(values):
    center = jnp.mean(values, axis=-1, keepdims=True)
    shifted = values - center
    spread = jnp.mean(shifted * shifted, axis=-1, keepdims=True)
    inverse = lax.rsqrt(spread + epsilon)
    return (shifted * inverse, inverse)


def mm(a, b, ca, cb):
    return lax.dot_general(a, b, (((ca,), (cb,)), ((), ())), preferred_element_type=f32)


def ring(size, step):
    return [(i, (i + step) % size) for i in range(size)]


def gather_pieces(piece, axis):
    size = lax.axis_size(axis)
    return [piece] + [lax.ppermute(piece, axis, ring(size, k)) for k in range(1, size)]


def in_order(pieces, axis):
    size = lax.axis_size(axis)
    own = lax.axis_index(axis)
    rows = pieces[0].shape[0]
    whole = jnp.zeros((size * rows,) + pieces[0].shape[1:], pieces[0].dtype)
    for k, piece in enumerate(pieces):
        place = lax.rem(own - k + size, size)
        whole = lax.dynamic_update_slice_in_dim(whole, piece, place * rows, 0)
    return whole


def scatter_total(parts, axis):
    size = lax.axis_size(axis)
    own = lax.axis_index(axis)
    rows = parts.shape[0] // size
    total = lax.dynamic_slice_in_dim(parts, own * rows, rows, 0).astype(f32)
    for k in range(1, size):
        place = lax.rem(own + k, size)
        block = lax.dynamic_slice_in_dim(parts, place * rows, rows, 0)
        total = total + lax.ppermute(block, axis, ring(size, k)).astype(f32)
    return total


def rotated(fields, cosine, sine):
    half = ROT // 2
    first = fields[:half]
    second = fields[half:ROT]
    return jnp.concatenate(
        [first * cosine - second * sine, second * cosine + first * sine, fields[ROT:]], axis=0
    )


def masked_block(low, high, block, row_ref, col_ref):
    same_doc = col_ref[:high] == row_ref[:, low : low + block]
    key_ids = lax.broadcasted_iota(jnp.int32, (high, block), 0)
    query_ids = low + lax.broadcasted_iota(jnp.int32, (high, block), 1)
    return same_doc & (key_ids <= query_ids)


def forward_kernel(qkv_ref, cos_ref, sin_ref, row_ref, col_ref, ctx_ref, turned_ref, total_ref):
    length = qkv_ref.shape[-1]
    block = min(256, length)
    cosine = cos_ref[...]
    sine = sin_ref[...]
    scale = 1.0 / math.sqrt(HEAD)
    query = (rotated(qkv_ref[0, 0], cosine, sine).astype(bf16).astype(f32) * scale).astype(bf16)
    keys = rotated(qkv_ref[1, 0], cosine, sine).astype(bf16)
    values = qkv_ref[2, 0].astype(bf16)
    turned_ref[0, 0] = query
    turned_ref[1, 0] = keys
    turned_ref[2, 0] = values
    for low in range(0, length, block):
        high = low + block
        scores = mm(keys[:, :high], query[:, low:high], 0, 0)
        scores = jnp.where(masked_block(low, high, block, row_ref, col_ref), scores, masked_score)
        peak = jnp.max(scores, axis=0, keepdims=True)
        terms = jnp.exp(scores - peak)
        total = jnp.sum(terms, axis=0, keepdims=True)
        probs = (terms * (1.0 / total)).astype(bf16)
        ctx_ref[0, :, low:high] = mm(values[:, :high], probs, 1, 0).astype(bf16)
        total_ref[0, :, low:high] = peak + jnp.log(total)


def backward_kernel(turned_ref, grad_ref, total_ref, cos_ref, sin_ref, row_ref, col_ref, out_ref):
    length = turned_ref.shape[-1]
    block = min(256, length)
    cosine = cos_ref[...]
    sine = -sin_ref[...]
    scale = 1.0 / math.sqrt(HEAD)
    query = turned_ref[0, 0]
    keys = turned_ref[1, 0]
    values = turned_ref[2, 0]
    grads = grad_ref[0]
    grad_query = []
    grad_key = [None] * (length // block)
    grad_value = [None] * (length // block)
    for index in range(length // block):
        low = index * block
        high = low + block
        query_block = query[:, low:high]
        grad_block = grads[:, low:high]
        scores = mm(keys[:, :high], query_block, 0, 0) - total_ref[0, :, low:high]
        scores = jnp.where(masked_block(low, high, block, row_ref, col_ref), scores, masked_score)
        probs = jnp.exp(scores)
        grad_probs = mm(values[:, :high], grad_block, 0, 0)
        delta = jnp.sum(probs * grad_probs, axis=0, keepdims=True)
        grad_scores = (probs * (grad_probs - delta)).astype(bf16)
        grad_query.append(mm(keys[:, :high], grad_scores, 1, 0) * scale)
        dk = mm(query_block, grad_scores, 1, 1)
        dv = mm(grad_block, probs.astype(bf16), 1, 1)
        for j in range(index + 1):
            part = slice(j * block, (j + 1) * block)
            grad_key[j] = dk[:, part] if grad_key[j] is None else grad_key[j] + dk[:, part]
            grad_value[j] = dv[:, part] if grad_value[j] is None else grad_value[j] + dv[:, part]
    out_ref[0, 0] = rotated(jnp.concatenate(grad_query, axis=1), cosine, sine).astype(bf16)
    out_ref[1, 0] = rotated(jnp.concatenate(grad_key, axis=1), cosine, sine).astype(bf16)
    out_ref[2, 0] = jnp.concatenate(grad_value, axis=1).astype(bf16)


def whole(shape):
    return pl.BlockSpec(shape, lambda h: (0,) * len(shape))


def three(head, length):
    return pl.BlockSpec((3, 1, head, length), lambda h: (0, h, 0, 0))


def one(head, length):
    return pl.BlockSpec((1, head, length), lambda h: (h, 0, 0))


def attend_forward(qkv, cosine, sine, row, col):
    _, heads, head, length = qkv.shape
    return pl.pallas_call(
        forward_kernel,
        grid=(heads,),
        in_specs=[three(head, length)] + [whole(item.shape) for item in (cosine, sine, row, col)],
        out_specs=[one(head, length), three(head, length), one(1, length)],
        out_shape=[
            jax.ShapeDtypeStruct((heads, head, length), bf16),
            jax.ShapeDtypeStruct((3, heads, head, length), bf16),
            jax.ShapeDtypeStruct((heads, 1, length), f32),
        ],
        name="attend_forward",
    )(qkv, cosine, sine, row, col)


def attend_backward(turned, grads, totals, cosine, sine, row, col):
    _, heads, head, length = turned.shape
    return pl.pallas_call(
        backward_kernel,
        grid=(heads,),
        in_specs=[three(head, length), one(head, length), one(1, length)]
        + [whole(item.shape) for item in (cosine, sine, row, col)],
        out_specs=three(head, length),
        out_shape=jax.ShapeDtypeStruct((3, heads, head, length), bf16),
        name="attend_backward",
    )(turned, grads, totals, cosine, sine, row, col)


def shards(
    layer_input,
    cotangent,
    segment_ids,
    positions,
    query_key_value_weight,
    projection_matrix,
    up_matrix,
    down_matrix,
    attn_gain,
    attn_shift,
    ffn_gain,
    ffn_shift,
    out_bias,
    up_projection_bias,
):
    fsdp_size = lax.axis_size("fsdp")
    ctx_size = lax.axis_size("ctx")
    tensor_size = lax.axis_size("tensor")
    ctx_own = lax.axis_index("ctx")
    tensor_own = lax.axis_index("tensor")
    _, piece_len, width = layer_input.shape
    seq_len = piece_len * ctx_size
    rows = query_key_value_weight.shape[0]
    head_count = HEADS // ctx_size
    head_width = head_count * HEAD
    half_tensor = FF // tensor_size
    units = half_tensor // ctx_size
    other_tensor = [(i, (i + 1) % tensor_size) for i in range(tensor_size)]

    head_start = ctx_own * head_width
    unit_start = lambda t: t * half_tensor + ctx_own * units
    other_own = tensor_size - 1 - tensor_own
    swap = lambda value: lax.ppermute(value, "tensor", other_tensor)

    piece = layer_input.reshape(piece_len, width)
    cot_piece = cotangent.reshape(piece_len, width)
    pieces = gather_pieces(piece, "ctx")
    labels = jnp.concatenate([segment_ids, positions], axis=0)
    label_pieces = gather_pieces(labels, "ctx")
    grad_bf = lax.all_gather(cot_piece, "ctx", axis=0, tiled=True)

    qkv_own = [
        lax.dynamic_slice_in_dim(query_key_value_weight, c * width + head_start, head_width, 1)
        for c in range(3)
    ]
    up_own = lax.dynamic_slice_in_dim(up_matrix, ctx_own * units, units, 1)
    down_own = lax.dynamic_slice_in_dim(down_matrix, ctx_own * units, units, 0).T
    edge = 3 * head_width
    small = jnp.concatenate(
        [attn_gain, attn_shift, ffn_gain, ffn_shift, out_bias, up_projection_bias]
    )
    small_rows = 16
    small = jnp.pad(small, (0, small_rows * (edge + units) - small.shape[0]))
    first_set = jnp.concatenate(
        [jnp.concatenate(qkv_own + [up_own], axis=1), small.reshape(small_rows, -1)], axis=0
    )
    first_pieces = gather_pieces(first_set, "fsdp")
    second_set = jnp.concatenate([down_own, projection_matrix], axis=1)
    second_pieces = gather_pieces(second_set, "fsdp")
    first_w = in_order([item[:rows] for item in first_pieces], "fsdp")
    qkv_w = first_w[:, :edge]
    up_half = first_w[:, edge:]
    up_w = jnp.concatenate([up_half, swap(up_half)], axis=1)
    second_w = in_order(second_pieces, "fsdp")
    down_half = second_w[:, :units]
    down_w = jnp.concatenate([down_half, swap(down_half)], axis=1)
    proj_w = lax.dynamic_slice_in_dim(second_w[:, units:], head_start, head_width, 0)
    small_len = 5 * rows + FF // fsdp_size
    vectors = in_order(
        [item[rows:].reshape(1, -1)[:, :small_len] for item in first_pieces], "fsdp"
    ).astype(f32)
    take = lambda k: vectors[:, k * rows : (k + 1) * rows].reshape(width)
    gain_one, shift_one, gain_two, shift_two, bias_all = [take(k) for k in range(5)]
    up_bias = vectors[:, 5 * rows :].reshape(FF)
    bias_w = jnp.concatenate(
        [
            lax.dynamic_slice_in_dim(up_bias, unit_start(tensor_own), units, 0),
            lax.dynamic_slice_in_dim(up_bias, unit_start(other_own), units, 0),
        ]
    )

    tokens = in_order(pieces, "ctx")
    all_labels = in_order([item[None] for item in label_pieces], "ctx")
    segment = all_labels[:, 0].reshape(seq_len)
    place = all_labels[:, 1].reshape(seq_len).astype(f32)
    half_rot = ROT // 2
    frequency = 10000.0 ** (-(2.0 * jnp.arange(half_rot, dtype=f32)) / ROT)
    angles = frequency[:, None] * place[None, :]
    tables = (jnp.cos(angles), jnp.sin(angles), segment[None, :], segment[:, None])

    normed, _ = normalize(tokens.astype(f32))
    first_hidden = (normed * gain_one + shift_one).astype(bf16)
    second_hidden = (normed * gain_two + shift_two).astype(bf16)
    qkv = mm(qkv_w, first_hidden, 0, 1).reshape(3, head_count, HEAD, seq_len)
    context, turned, totals = attend_forward(qkv, *tables)
    context = context.reshape(head_width, seq_len)
    pre = mm(second_hidden, up_w, 1, 0) + bias_w
    cdf = 0.5 * (1.0 + lax.erf(pre * (1.0 / math.sqrt(2.0))))
    act = (pre * cdf).astype(bf16)
    slope = (cdf + pre * (jnp.exp(-0.5 * pre * pre) * (1.0 / math.sqrt(2.0 * math.pi)))).astype(bf16)
    out_part = (mm(act, down_w, 1, 1) + mm(context, proj_w, 0, 0)).astype(bf16)
    grad_bf, out_part = lax.optimization_barrier((grad_bf, out_part))
    out_sum = lax.psum_scatter(out_part, "ctx", scatter_dimension=0, tiled=True).astype(f32)
    output = piece.astype(f32) + out_sum + bias_all
    layer_output = output.astype(bf16)[None]

    grad_pre = (mm(grad_bf, down_w, 1, 0) * slope.astype(f32)).astype(bf16)
    up_part = mm(second_hidden, grad_pre, 0, 0)
    down_part = mm(grad_bf, act, 0, 0)
    proj_part = mm(grad_bf, context, 0, 1)
    half_width = head_width // tensor_size
    proj_keep = lax.dynamic_slice_in_dim(proj_part, tensor_own * half_width, half_width, 1)
    proj_send = lax.dynamic_slice_in_dim(proj_part, other_own * half_width, half_width, 1)
    ffn_keep = jnp.concatenate([up_part[:, :units], down_part[:, :units], proj_keep], axis=1)
    ffn_send = jnp.concatenate([up_part[:, units:], down_part[:, units:], proj_send], axis=1)
    ffn_grad = (ffn_keep + swap(ffn_send.astype(bf16)).astype(f32)).astype(bf16)
    ffn_rows = scatter_total(ffn_grad, "fsdp").astype(bf16)
    ffn_all = lax.all_gather(ffn_rows, "ctx", axis=0, tiled=False)
    up_grad = jnp.concatenate([ffn_all[z, :, :units] for z in range(ctx_size)], axis=1).astype(f32)
    down_grad = ffn_all[:, :, units : 2 * units].transpose(0, 2, 1).reshape(half_tensor, rows)
    down_grad = down_grad.astype(f32)
    proj_half = ffn_all[:, :, 2 * units :].transpose(0, 2, 1)
    proj_other = swap(proj_half)
    proj_cols = jnp.where(
        tensor_own == 0,
        jnp.concatenate([proj_half, proj_other], axis=1),
        jnp.concatenate([proj_other, proj_half], axis=1),
    )
    proj_grad = lax.all_to_all(proj_cols.reshape(fsdp_size, rows, rows), "fsdp", 0, 0, tiled=True)
    proj_grad = jnp.concatenate([proj_grad[f] for f in range(fsdp_size)], axis=1).astype(f32)

    grad_context = mm(proj_w, grad_bf, 1, 1).astype(bf16).reshape(head_count, HEAD, seq_len)
    grad_projected = attend_backward(turned, grad_context, totals, *tables)
    grad_projected = grad_projected.reshape(edge, seq_len)
    grad_two = mm(grad_pre, up_w, 1, 1)
    grad_one = mm(grad_projected, qkv_w, 0, 1)
    mixed = (grad_one * gain_one + grad_two * gain_two).astype(bf16)
    scaled = scatter_total(mixed, "ctx")
    own_normed, own_inverse = normalize(piece.astype(f32))
    first_mean = jnp.mean(scaled, axis=-1, keepdims=True)
    second_mean = jnp.mean(scaled * own_normed, axis=-1, keepdims=True)
    cot_float = cot_piece.astype(f32)
    input_grad = cot_float + own_inverse * (scaled - first_mean - own_normed * second_mean)

    qkv_part = mm(first_hidden, grad_projected, 0, 1)
    bias_sum = jnp.sum(grad_pre.astype(f32), axis=0)
    bias_part = jnp.zeros((FF,), f32)
    bias_part = lax.dynamic_update_slice_in_dim(bias_part, bias_sum[:units], unit_start(tensor_own), 0)
    bias_part = lax.dynamic_update_slice_in_dim(bias_part, bias_sum[units:], unit_start(other_own), 0)
    small_part = jnp.stack(
        [
            jnp.sum(grad_one * normed, axis=0),
            jnp.sum(grad_one, axis=0),
            jnp.sum(grad_two * normed, axis=0),
            jnp.sum(grad_two, axis=0),
            jnp.sum(cot_float, axis=0),
        ],
        axis=1,
    )
    attn_part = jnp.concatenate(
        [qkv_part, small_part, bias_part.reshape(width, FF // width)], axis=1
    )
    sub = rows // tensor_size
    attn_part = attn_part.reshape(fsdp_size, tensor_size, sub, -1)
    attn_keep = lax.dynamic_index_in_dim(attn_part, tensor_own, 1, keepdims=False)
    attn_send = lax.dynamic_index_in_dim(attn_part, other_own, 1, keepdims=False).astype(bf16)
    attn_grad = (attn_keep + swap(attn_send).astype(f32)).astype(bf16)
    attn_rows = scatter_total(attn_grad.reshape(fsdp_size * sub, -1), "fsdp").astype(bf16)
    attn_half = in_order([item[None] for item in gather_pieces(attn_rows, "ctx")], "ctx")
    attn_other = swap(attn_half)
    attn_low = jnp.where(tensor_own == 0, attn_half, attn_other).astype(f32)
    attn_high = jnp.where(tensor_own == 0, attn_other, attn_half).astype(f32)
    spread = lambda item: jnp.concatenate(
        [
            item[z, :, c * head_width : (c + 1) * head_width]
            for c in range(3)
            for z in range(ctx_size)
        ],
        axis=1,
    )
    qkv_grad = jnp.concatenate([spread(attn_low), spread(attn_high)], axis=0)
    tail = jnp.concatenate(
        [jnp.sum(attn_low[:, :, edge:], axis=0), jnp.sum(attn_high[:, :, edge:], axis=0)], axis=0
    )
    bias_grad = tail[:, 5:].reshape(FF // fsdp_size)
    return (
        layer_output,
        input_grad[None],
        qkv_grad,
        proj_grad,
        up_grad,
        down_grad,
        tail[:, 0],
        tail[:, 1],
        tail[:, 2],
        tail[:, 3],
        tail[:, 4],
        bias_grad,
    )


def solution(mesh):
    tokens = P(("fsdp", "tensor"), "ctx", None)
    labels = P(("fsdp", "tensor"), "ctx")
    weights = (P("fsdp", None), P("fsdp", None), P("fsdp", "tensor"), P("tensor", "fsdp"))
    vectors = (P("fsdp"),) * 6
    return jax.shard_map(
        shards,
        mesh=mesh,
        in_specs=(tokens, tokens, labels, labels) + weights + vectors,
        out_specs=(tokens, tokens) + weights + vectors,
        check_vma=False,
    )
```

```python
import math

import jax
import jax.numpy as jnp
from jax import lax
from jax.experimental import pallas as pl
from jax.sharding import PartitionSpec as P


HEADS = 12
HEAD = 64
ROT = 16
FF = 3072

epsilon = 1e-05
masked_score = -1e30
bf16 = jnp.bfloat16
f32 = jnp.float32


def normalize(values):
    center = jnp.mean(values, axis=-1, keepdims=True)
    shifted = values - center
    spread = jnp.mean(shifted * shifted, axis=-1, keepdims=True)
    inverse = lax.rsqrt(spread + epsilon)
    return (shifted * inverse, inverse)


def mm(a, b, ca, cb):
    return lax.dot_general(a, b, (((ca,), (cb,)), ((), ())), preferred_element_type=f32)


def ring(size, step):
    return [(i, (i + step) % size) for i in range(size)]


def gather_pieces(piece, axis):
    size = lax.axis_size(axis)
    return [piece] + [lax.ppermute(piece, axis, ring(size, k)) for k in range(1, size)]


def in_order(pieces, axis):
    size = len(pieces)
    shape = (size,) + (1,) * pieces[0].ndim
    source = lax.rem(lax.axis_index(axis) - jnp.arange(size) + size, size).reshape(shape)
    whole = jnp.where(source == 0, pieces[0][None], pieces[1][None])
    for k in range(2, size):
        whole = jnp.where(source == k, pieces[k][None], whole)
    return whole


def scatter_total(parts, axis):
    size = lax.axis_size(axis)
    own = lax.axis_index(axis)
    rows = parts.shape[0] // size
    total = lax.dynamic_slice_in_dim(parts, own * rows, rows, 0).astype(f32)
    for k in range(1, size):
        place = lax.rem(own + k, size)
        block = lax.dynamic_slice_in_dim(parts, place * rows, rows, 0)
        total = total + lax.ppermute(block, axis, ring(size, k)).astype(f32)
    return total


def rotated(fields, cosine, sine):
    half = ROT // 2
    first = fields[:half]
    second = fields[half:ROT]
    return jnp.concatenate(
        [first * cosine - second * sine, second * cosine + first * sine, fields[ROT:]], axis=0
    )


def masked_block(low, high, block, row_ref, col_ref):
    same_doc = col_ref[:high] == row_ref[:, low : low + block]
    key_ids = lax.broadcasted_iota(jnp.int32, (high, block), 0)
    query_ids = low + lax.broadcasted_iota(jnp.int32, (high, block), 1)
    return same_doc & (key_ids <= query_ids)


def forward_kernel(qkv_ref, cos_ref, sin_ref, row_ref, col_ref, ctx_ref, turned_ref, total_ref):
    length = qkv_ref.shape[-1]
    block = min(256, length)
    cosine = cos_ref[...]
    sine = sin_ref[...]
    scale = 1.0 / math.sqrt(HEAD)
    query = (rotated(qkv_ref[0, 0], cosine, sine).astype(bf16).astype(f32) * scale).astype(bf16)
    keys = rotated(qkv_ref[1, 0], cosine, sine).astype(bf16)
    values = qkv_ref[2, 0].astype(bf16)
    turned_ref[0, 0] = query
    turned_ref[1, 0] = keys
    turned_ref[2, 0] = values
    for low in range(0, length, block):
        high = low + block
        scores = mm(keys[:, :high], query[:, low:high], 0, 0)
        scores = jnp.where(masked_block(low, high, block, row_ref, col_ref), scores, masked_score)
        peak = jnp.max(scores, axis=0, keepdims=True)
        terms = jnp.exp(scores - peak)
        total = jnp.sum(terms, axis=0, keepdims=True)
        probs = (terms * (1.0 / total)).astype(bf16)
        ctx_ref[0, :, low:high] = mm(values[:, :high], probs, 1, 0).astype(bf16)
        total_ref[0, :, low:high] = peak + jnp.log(total)


def backward_kernel(turned_ref, grad_ref, total_ref, cos_ref, sin_ref, row_ref, col_ref, out_ref):
    length = turned_ref.shape[-1]
    block = min(256, length)
    cosine = cos_ref[...]
    sine = -sin_ref[...]
    scale = 1.0 / math.sqrt(HEAD)
    query = turned_ref[0, 0]
    keys = turned_ref[1, 0]
    values = turned_ref[2, 0]
    grads = grad_ref[0]
    grad_query = []
    grad_key = [None] * (length // block)
    grad_value = [None] * (length // block)
    for index in range(length // block):
        low = index * block
        high = low + block
        query_block = query[:, low:high]
        grad_block = grads[:, low:high]
        scores = mm(keys[:, :high], query_block, 0, 0) - total_ref[0, :, low:high]
        scores = jnp.where(masked_block(low, high, block, row_ref, col_ref), scores, masked_score)
        probs = jnp.exp(scores)
        grad_probs = mm(values[:, :high], grad_block, 0, 0)
        delta = jnp.sum(probs * grad_probs, axis=0, keepdims=True)
        grad_scores = (probs * (grad_probs - delta)).astype(bf16)
        grad_query.append(mm(keys[:, :high], grad_scores, 1, 0) * scale)
        dk = mm(query_block, grad_scores, 1, 1)
        dv = mm(grad_block, probs.astype(bf16), 1, 1)
        for j in range(index + 1):
            part = slice(j * block, (j + 1) * block)
            grad_key[j] = dk[:, part] if grad_key[j] is None else grad_key[j] + dk[:, part]
            grad_value[j] = dv[:, part] if grad_value[j] is None else grad_value[j] + dv[:, part]
    out_ref[0, 0] = rotated(jnp.concatenate(grad_query, axis=1), cosine, sine).astype(bf16)
    out_ref[1, 0] = rotated(jnp.concatenate(grad_key, axis=1), cosine, sine).astype(bf16)
    out_ref[2, 0] = jnp.concatenate(grad_value, axis=1).astype(bf16)


def whole(shape):
    return pl.BlockSpec(shape, lambda h: (0,) * len(shape))


def three(head, length):
    return pl.BlockSpec((3, 1, head, length), lambda h: (0, h, 0, 0))


def one(head, length):
    return pl.BlockSpec((1, head, length), lambda h: (h, 0, 0))


def attend_forward(qkv, cosine, sine, row, col):
    _, heads, head, length = qkv.shape
    return pl.pallas_call(
        forward_kernel,
        grid=(heads,),
        in_specs=[three(head, length)] + [whole(item.shape) for item in (cosine, sine, row, col)],
        out_specs=[one(head, length), three(head, length), one(1, length)],
        out_shape=[
            jax.ShapeDtypeStruct((heads, head, length), bf16),
            jax.ShapeDtypeStruct((3, heads, head, length), bf16),
            jax.ShapeDtypeStruct((heads, 1, length), f32),
        ],
        name="attend_forward",
    )(qkv, cosine, sine, row, col)


def attend_backward(turned, grads, totals, cosine, sine, row, col):
    _, heads, head, length = turned.shape
    return pl.pallas_call(
        backward_kernel,
        grid=(heads,),
        in_specs=[three(head, length), one(head, length), one(1, length)]
        + [whole(item.shape) for item in (cosine, sine, row, col)],
        out_specs=three(head, length),
        out_shape=jax.ShapeDtypeStruct((3, heads, head, length), bf16),
        name="attend_backward",
    )(turned, grads, totals, cosine, sine, row, col)


def shards(
    layer_input,
    cotangent,
    segment_ids,
    positions,
    query_key_value_weight,
    projection_matrix,
    up_matrix,
    down_matrix,
    attn_gain,
    attn_shift,
    ffn_gain,
    ffn_shift,
    out_bias,
    up_projection_bias,
):
    fsdp_size = lax.axis_size("fsdp")
    ctx_size = lax.axis_size("ctx")
    tensor_size = lax.axis_size("tensor")
    ctx_own = lax.axis_index("ctx")
    tensor_own = lax.axis_index("tensor")
    _, piece_len, width = layer_input.shape
    seq_len = piece_len * ctx_size
    rows = query_key_value_weight.shape[0]
    head_count = HEADS // ctx_size
    head_width = head_count * HEAD
    half_tensor = FF // tensor_size
    units = half_tensor // ctx_size
    other_tensor = [(i, (i + 1) % tensor_size) for i in range(tensor_size)]

    head_start = ctx_own * head_width
    unit_start = lambda t: t * half_tensor + ctx_own * units
    other_own = tensor_size - 1 - tensor_own
    swap = lambda value: lax.ppermute(value, "tensor", other_tensor)

    piece = layer_input.reshape(piece_len, width)
    cot_piece = cotangent.reshape(piece_len, width)
    pieces = gather_pieces(piece, "ctx")
    label_pieces = gather_pieces(segment_ids, "ctx")
    barred = lax.optimization_barrier((cot_piece, *pieces))
    cot_piece, pieces = barred[0], barred[1:]
    cot_pieces = gather_pieces(cot_piece, "ctx")

    qkv_own = [
        lax.dynamic_slice_in_dim(query_key_value_weight, c * width + head_start, head_width, 1)
        for c in range(3)
    ]
    up_own = lax.dynamic_slice_in_dim(up_matrix, ctx_own * units, units, 1)
    down_own = lax.dynamic_slice_in_dim(down_matrix, ctx_own * units, units, 0).T
    edge = 3 * head_width
    first_set = jnp.concatenate(qkv_own + [up_own], axis=1)
    second_set = jnp.concatenate([down_own, projection_matrix], axis=1)
    vector_row = lambda item: jnp.pad(item[None], ((0, 0), (0, width - item.shape[0])))
    small = [attn_gain, attn_shift, ffn_gain, ffn_shift, out_bias, up_projection_bias]
    blank = jnp.zeros((8 - len(small), width), bf16)
    small = jnp.concatenate([vector_row(item) for item in small] + [blank], axis=0)
    first_all = gather_pieces(first_set, "fsdp")
    second_all = gather_pieces(second_set, "fsdp")
    small_all = gather_pieces(small, "fsdp")
    qkv_w = in_order([item[:, :edge] for item in first_all], "fsdp").reshape(width, edge)
    up_half = in_order([item[:, edge:] for item in first_all], "fsdp").reshape(width, units)
    up_w = jnp.concatenate([up_half, swap(up_half)], axis=1)
    down_half = in_order([item[:, :units] for item in second_all], "fsdp").reshape(width, units)
    down_w = jnp.concatenate([down_half, swap(down_half)], axis=1)
    proj_all = in_order([item[:, units:] for item in second_all], "fsdp").reshape(width, width)
    proj_w = lax.dynamic_slice_in_dim(proj_all, head_start, head_width, 0)
    vectors = in_order(small_all, "fsdp")
    up_bias = vectors[:, 5, : FF // fsdp_size].reshape(FF).astype(f32)
    vectors = vectors[:, :, :rows].transpose(1, 0, 2).reshape(8, width).astype(f32)
    gain_one, shift_one, gain_two, shift_two, bias_all = [vectors[k : k + 1] for k in range(5)]
    bias_w = jnp.concatenate(
        [
            lax.dynamic_slice_in_dim(up_bias, unit_start(tensor_own), units, 0),
            lax.dynamic_slice_in_dim(up_bias, unit_start(other_own), units, 0),
        ]
    )

    tokens = in_order(pieces, "ctx").reshape(seq_len, width)
    segment = in_order(label_pieces, "ctx").reshape(seq_len)
    earlier = jnp.sum((segment[None, :] < segment[:, None]).astype(f32), axis=1)
    place = jnp.arange(seq_len, dtype=f32) - earlier
    half_rot = ROT // 2
    frequency = 10000.0 ** (-(2.0 * jnp.arange(half_rot, dtype=f32)) / ROT)
    angles = frequency[:, None] * place[None, :]
    tables = (jnp.cos(angles), jnp.sin(angles), segment[None, :], segment[:, None])

    normed, _ = normalize(tokens.astype(f32))
    first_hidden = (normed * gain_one + shift_one).astype(bf16)
    second_hidden = (normed * gain_two + shift_two).astype(bf16)
    qkv = mm(qkv_w, first_hidden, 0, 1).reshape(3, head_count, HEAD, seq_len)
    context, turned, totals = attend_forward(qkv, *tables)
    context = context.reshape(head_width, seq_len)
    pre = mm(second_hidden, up_w, 1, 0) + bias_w
    cdf = 0.5 * (1.0 + lax.erf(pre * (1.0 / math.sqrt(2.0))))
    act = (pre * cdf).astype(bf16)
    slope = (cdf + pre * (jnp.exp(-0.5 * pre * pre) * (1.0 / math.sqrt(2.0 * math.pi)))).astype(bf16)
    out_part = (mm(act, down_w, 1, 1) + mm(context, proj_w, 0, 0)).astype(bf16)
    cot_sum = jnp.sum(cot_piece.astype(f32), axis=0)
    cot_sum, out_part = lax.optimization_barrier((cot_sum, out_part))
    out_sum = scatter_total(out_part, "ctx")
    grad_bf = in_order(cot_pieces, "ctx").reshape(seq_len, width)
    output = piece.astype(f32) + out_sum + bias_all
    layer_output = output.astype(bf16)[None]

    grad_pre = (mm(grad_bf, down_w, 1, 0) * slope.astype(f32)).astype(bf16)
    up_part = mm(second_hidden, grad_pre, 0, 0)
    down_part = mm(grad_bf, act, 0, 0)
    proj_part = mm(grad_bf, context, 0, 1)
    half_width = head_width // tensor_size
    proj_keep = lax.dynamic_slice_in_dim(proj_part, tensor_own * half_width, half_width, 1)
    proj_send = lax.dynamic_slice_in_dim(proj_part, other_own * half_width, half_width, 1)
    ffn_keep = jnp.concatenate([up_part[:, :units], down_part[:, :units], proj_keep], axis=1)
    ffn_send = jnp.concatenate([up_part[:, units:], down_part[:, units:], proj_send], axis=1)
    ffn_grad = (ffn_keep + swap(ffn_send.astype(bf16)).astype(f32)).astype(bf16)
    ffn_rows = scatter_total(ffn_grad, "fsdp").astype(bf16)
    ffn_all = in_order(gather_pieces(ffn_rows, "ctx"), "ctx")
    up_grad = jnp.concatenate([ffn_all[z, :, :units] for z in range(ctx_size)], axis=1).astype(f32)
    down_grad = ffn_all[:, :, units : 2 * units].transpose(0, 2, 1).reshape(half_tensor, rows)
    down_grad = down_grad.astype(f32)
    proj_half = ffn_all[:, :, 2 * units :].transpose(0, 2, 1)
    proj_other = swap(proj_half)
    proj_cols = jnp.where(
        tensor_own == 0,
        jnp.concatenate([proj_half, proj_other], axis=1),
        jnp.concatenate([proj_other, proj_half], axis=1),
    )
    proj_grad = lax.all_to_all(proj_cols.reshape(fsdp_size, rows, rows), "fsdp", 0, 0, tiled=True)
    proj_grad = jnp.concatenate([proj_grad[f] for f in range(fsdp_size)], axis=1).astype(f32)

    grad_context = mm(proj_w, grad_bf, 1, 1).astype(bf16).reshape(head_count, HEAD, seq_len)
    grad_projected = attend_backward(turned, grad_context, totals, *tables)
    grad_projected = grad_projected.reshape(edge, seq_len)
    grad_two = mm(grad_pre, up_w, 1, 1)
    grad_one = mm(grad_projected, qkv_w, 0, 1)
    mixed = (grad_one * gain_one + grad_two * gain_two).astype(bf16)
    scaled = scatter_total(mixed, "ctx")
    own_normed, own_inverse = normalize(piece.astype(f32))
    first_mean = jnp.mean(scaled, axis=-1, keepdims=True)
    second_mean = jnp.mean(scaled * own_normed, axis=-1, keepdims=True)
    cot_float = cot_piece.astype(f32)
    input_grad = cot_float + own_inverse * (scaled - first_mean - own_normed * second_mean)

    qkv_part = mm(first_hidden, grad_projected, 0, 1)
    qkv_part, _ = lax.optimization_barrier((qkv_part, ffn_rows))
    bias_sum = jnp.sum(grad_pre.astype(f32), axis=0)
    bias_part = jnp.zeros((FF,), f32)
    bias_part = lax.dynamic_update_slice_in_dim(bias_part, bias_sum[:units], unit_start(tensor_own), 0)
    bias_part = lax.dynamic_update_slice_in_dim(bias_part, bias_sum[units:], unit_start(other_own), 0)
    small_part = jnp.stack(
        [
            jnp.sum(grad_one * normed, axis=0),
            jnp.sum(grad_one, axis=0),
            jnp.sum(grad_two * normed, axis=0),
            jnp.sum(grad_two, axis=0),
            cot_sum,
        ]
    )
    small_part = small_part.reshape(5, fsdp_size, rows).transpose(1, 0, 2)
    bias_part = bias_part.reshape(fsdp_size, FF // width, rows)
    extra = 8
    fill = lambda item: jnp.pad(
        item, ((0, 0), (0, extra - item.shape[1]), (0, edge - rows))
    )[:, None]
    small_part = jnp.concatenate([fill(small_part), fill(bias_part)], axis=1)
    sub = rows // tensor_size
    qkv_part = qkv_part.reshape(fsdp_size, tensor_size, sub, edge)
    pick = lambda t: jnp.concatenate(
        [
            lax.dynamic_index_in_dim(qkv_part, t, 1, keepdims=False),
            lax.dynamic_index_in_dim(small_part, t, 1, keepdims=False),
        ],
        axis=1,
    )
    attn_grad = (pick(tensor_own) + swap(pick(other_own).astype(bf16)).astype(f32)).astype(bf16)
    attn_rows = scatter_total(attn_grad.reshape(fsdp_size * (sub + extra), edge), "fsdp")
    attn_rows = attn_rows.astype(bf16)
    attn_half = in_order(gather_pieces(attn_rows, "ctx"), "ctx")
    attn_other = swap(attn_half)
    attn_low = jnp.where(tensor_own == 0, attn_half, attn_other).astype(f32)
    attn_high = jnp.where(tensor_own == 0, attn_other, attn_half).astype(f32)
    spread = lambda item: jnp.concatenate(
        [
            item[z, :sub, c * head_width : (c + 1) * head_width]
            for c in range(3)
            for z in range(ctx_size)
        ],
        axis=1,
    )
    qkv_grad = jnp.concatenate([spread(attn_low), spread(attn_high)], axis=0)
    tail = jnp.sum(attn_low[:, sub:, :rows], axis=0)
    bias_grad = jnp.sum(attn_high[:, sub:, :rows], axis=0)[: FF // width].reshape(FF // fsdp_size)
    return (
        layer_output,
        input_grad[None],
        qkv_grad,
        proj_grad,
        up_grad,
        down_grad,
        tail[0],
        tail[1],
        tail[2],
        tail[3],
        tail[4],
        bias_grad,
    )


def solution(mesh):
    tokens = P(("fsdp", "tensor"), "ctx", None)
    labels = P(("fsdp", "tensor"), "ctx")
    weights = (P("fsdp", None), P("fsdp", None), P("fsdp", "tensor"), P("tensor", "fsdp"))
    vectors = (P("fsdp"),) * 6

    return jax.shard_map(
        shards,
        mesh=mesh,
        in_specs=(tokens, tokens, labels, labels) + weights + vectors,
        out_specs=(tokens, tokens) + weights + vectors,
        check_vma=False,
    )
```
